256 devices in a mesh: pairs: 64 (over z, y, core), cols: 4 (over x).
Axes of the slice: x: 4, y: 4, z: 8, core: 2. Of those that a mesh axis runs over, the one named last changes fastest.
Arguments:
- state: float32 [2, 64, 64, 16384], P(None, 'pairs', None, 'cols'), may hold values from -6 to 6
- sector_mix: float32 [127, 64, 64], P(None, None, 'cols'), may hold values from -2 to 2
- kerr_rates: float32 [2], replicated, may hold values from 0.002 to 0.02
- column_load: int32 [16384], P('cols'), may hold values from 0 to 255
Outputs:
- evolved: float32 [2, 64, 64, 16384], P(None, 'pairs', None, 'cols')
- moment: float32 [1], replicated
The draws below stay inside these ranges and needn't reach their ends.
All inputs are finite; a program needn't handle non-finite values.
Results may differ from the reference program's by a relative error of at most 0.0003.
Values sent between devices are 32-bit elements; how exact they have to be, the bound alone decides.
No kernel may reach another device: no remote copies, remote signals or barrier semaphores. Data moves between devices by JAX's collectives and lax.ppermute only.
A program may use at most 128 MiB of HBM per device.

```python
import math
import jax
import jax.numpy as jnp
import numpy as np
from jax import lax

OPT = 64
THIRD = 64
MEMB = 128
WINDOW = 2
COLS = 16384
SECTORS = 127


def draw_sector_mix(key, part):
    key_off, key_diag = jax.random.split(key, 2)
    shape = (SECTORS, OPT, OPT)
    sector_ids = lax.broadcasted_iota(jnp.int32, shape, 0)
    row_ids = lax.broadcasted_iota(jnp.int32, shape, 1)
    col_ids = lax.broadcasted_iota(jnp.int32, shape, 2)
    sector_size = jnp.minimum(sector_ids, SECTORS - 1 - sector_ids) + 1
    spread = 0.6 / jnp.sqrt(sector_size.astype(jnp.float32))
    off_diagonal = jax.random.normal(key_off, shape, jnp.float32) * spread
    off_diagonal = jnp.clip(off_diagonal, -3.0 * spread, 3.0 * spread)
    diagonal = 1.0 + 0.25 * jax.random.uniform(key_diag, shape, jnp.float32, -1.0, 1.0)
    return jnp.where(row_ids == col_ids, diagonal, off_diagonal)


def plant(entries, rng, least, largest):
    longest = entries.shape.index(max(entries.shape))
    spots = []
    for shift in (0, 1):
        where = [jax.random.randint(jax.random.fold_in(rng, axis), (), 0, length) for axis, length in enumerate(entries.shape)]
        where[longest] = (where[longest] + shift) % entries.shape[longest]
        spots.append(tuple(where))
    return entries.at[spots[0]].set(least).at[spots[1]].set(largest)


def shard_levels(key, extent, shards, smallest, high):
    level = 1.0
    for position, blocks in shards:
        steps = jax.random.uniform(jax.random.fold_in(jax.random.fold_in(key, 6), position), (blocks,), jnp.float32, smallest / len(shards), high / len(shards))
        level = level * jnp.repeat(jnp.exp(steps), extent[position] // blocks).reshape((-1,) + (1,) * (len(extent) - 1 - position))
    return level


def bell_draw(rng, dims, scale, reach, cuts=(), kind=jnp.bfloat16):
    drawn = scale * jax.random.normal(rng, dims, jnp.float32)
    if cuts:
        drawn = drawn * shard_levels(rng, dims, cuts, -0.22, 0.18)
    return jnp.clip(drawn, -reach, reach).astype(kind)


def setup_inputs(seed: int = 0) -> dict:
    seeds = jax.random.split(jax.random.key(seed), 5)
    return {
        "state": bell_draw(seeds[0], (2, OPT, OPT, COLS), 1.0, 6.0, ((1, 64), (3, 4)), jnp.float32),
        "sector_mix": draw_sector_mix(jax.random.fold_in(seeds[4], 71), 0),
        "kerr_rates": jnp.clip(jnp.exp(jax.random.uniform(seeds[2], (2,), jnp.float32, math.log(0.002), math.log(0.02))), 0.002, 0.02),
        "column_load": plant(jax.random.randint(seeds[3], (COLS,), 0, 256), jax.random.fold_in(seeds[3], 1), 0, 255).astype(jnp.int32),
    }


def sector_states(sector):
    low_end = max(0, sector - OPT + 1)
    high_end = min(sector, OPT - 1)
    return np.arange(low_end, high_end + 1)


def reference(state, sector_mix, kerr_rates, column_load):
    flat_state = state.reshape(2, OPT * OPT, COLS)
    pieces = []
    row_lists = []
    for sector in range(SECTORS):
        photon_one = sector_states(sector)
        sector_size = photon_one.shape[0]
        row_ids = (photon_one * OPT + sector - photon_one).astype(np.int32)
        sector_rows = jnp.take(flat_state, jnp.asarray(row_ids), axis=1)
        matrix = sector_mix[sector, :sector_size, :sector_size]
        pieces.append(jnp.einsum("ij,pjc->pic", matrix, sector_rows, precision=lax.Precision.HIGHEST))
        row_lists.append(row_ids)
    stacked = jnp.concatenate(pieces, axis=1)
    inverse = np.argsort(np.concatenate(row_lists)).astype(np.int32)
    mixed = jnp.take(stacked, jnp.asarray(inverse), axis=1).reshape(2, OPT, OPT, COLS)
    real_part = mixed[0]
    imag_part = mixed[1]
    levels = jnp.arange(OPT).astype(jnp.float32)
    loads = column_load.astype(jnp.float32)
    phases = (kerr_rates[0] * levels[:, None] + kerr_rates[1] * levels[None, :])[:, :, None] * loads[None, None, :]
    cosine = jnp.cos(phases)
    sine_part = jnp.sin(phases)
    evolved = jnp.stack([cosine * real_part - sine_part * imag_part, sine_part * real_part + cosine * imag_part])
    third_level = (jnp.arange(COLS) // (MEMB * WINDOW)).astype(jnp.float32)
    weight = (levels + 1.0)[:, None, None] * (third_level + 1.0)[None, None, :]
    summed = jnp.sum(weight * (real_part * real_part + imag_part * imag_part))
    moment = summed / float(OPT * OPT * COLS * OPT * THIRD)
    return evolved, moment.reshape(1)
```

```python
import functools

import jax
import jax.numpy as jnp
from jax import lax
from jax.experimental import pallas as pl
from jax.experimental.pallas import tpu as pltpu
from jax.sharding import PartitionSpec as P

THIRD = 64
MEMB = 128
WINDOW = 2
LEVELS = 64
LANES = 128
CHUNKS = 2


def blend(low, high, shift):
    sub = lax.broadcasted_iota(jnp.int32, low.shape, 0)
    return jnp.where(sub < shift, low, high)


def pack_kernel(x_ref, out_ref):
    blocks = x_ref.shape[2] // LANES
    lines = 2 * blocks
    n1 = lax.axis_index("pairs")
    tile, shift = n1 // 8, n1 % 8
    for part in range(2):
        for j in range(blocks):
            lanes = slice(j * LANES, (j + 1) * LANES)
            turned = [
                pltpu.roll(x_ref[part, 8 * a : 8 * a + 8, lanes], shift, 0) for a in range(LEVELS // 8)
            ]
            for a in range(LEVELS // 8):
                slot = 8 * ((a + tile) % 8)
                out_ref[pl.ds(slot * lines + part * blocks + j, 8, stride=lines), :] = blend(
                    turned[a - 1], turned[a], shift
                )


def mix_kernel(first_col, x_ref, pieces_ref, out_ref, moment_ref):
    lines = out_ref.shape[0] // LEVELS
    blocks = lines // 2
    owner = lax.axis_index("pairs")
    base = lax.axis_index("cols") * (4096 // 256)
    row = lax.broadcasted_iota(jnp.int32, (LEVELS, LANES), 0)
    col = lax.broadcasted_iota(jnp.int32, (LEVELS, LANES), 1)
    low = pieces_ref[0]
    high = pltpu.roll(pltpu.roll(pieces_ref[1], owner + 1, 0), owner + 1, 1)
    zero = jnp.zeros_like(low)
    low = jnp.where((row <= owner) & (col <= owner), low, zero)
    high = jnp.where((row > owner) & (col > owner) & (col < LEVELS), high, zero)
    matrix = (low + high)[:, :LEVELS]
    total = jnp.zeros((LEVELS, LANES), jnp.float32)
    for line in range(lines):
        mixed = jnp.dot(
            matrix,
            x_ref[pl.ds(line, LEVELS, stride=lines), :],
            precision=lax.Precision.HIGHEST,
            preferred_element_type=jnp.float32,
        )
        out_ref[pl.ds(line, LEVELS, stride=lines), :] = mixed
        third = base + (first_col + (line % blocks) * LANES) // (MEMB * WINDOW)
        total += (third + 1).astype(jnp.float32) * (mixed * mixed)
    moment_ref[...] = jnp.sum(total * (row + 1).astype(jnp.float32), axis=0, keepdims=True)


def turn_kernel(first, x_ref, cos_ref, sin_ref, *refs):
    out_ref = refs[-1]
    blocks = out_ref.shape[2] // LANES
    lines = 2 * blocks
    n1 = lax.axis_index("pairs")
    tile, shift = n1 // 8, n1 % 8
    back = (8 - shift) % 8

    def rows(part, j):
        turned = []
        for a in range(LEVELS // 8 + 1):
            slot = 8 * ((a + tile) % 8)
            turned.append(
                pltpu.roll(x_ref[pl.ds(slot * lines + part * blocks + j, 8, stride=lines), :], back, 0)
            )
        return [blend(turned[a], turned[a + 1], 8 - shift) for a in range(LEVELS // 8)]

    for j in range(blocks):
        lanes = slice(j * LANES, (j + 1) * LANES)
        real, imag = rows(0, j), rows(1, j)
        for a in range(LEVELS // 8):
            span = slice(8 * a, 8 * a + 8)
            cosine, sine = cos_ref[span, lanes], sin_ref[span, lanes]
            out_ref[0, span, lanes] = cosine * real[a] - sine * imag[a]
            out_ref[1, span, lanes] = sine * real[a] + cosine * imag[a]


def local(state, sector_mix, kerr_rates, column_load):
    pair_count = lax.axis_size("pairs")
    col_devices = lax.axis_size("cols")
    device = lax.axis_index("pairs")
    col_device = lax.axis_index("cols")
    levels, col_count = state.shape[2], state.shape[3]
    assert pair_count == levels == LEVELS and state.shape[1] == 1
    state = state.reshape(2, levels, col_count)
    width = col_count // CHUNKS
    blocks = width // LANES
    lines = 2 * blocks
    size = levels * lines
    vmem = pl.BlockSpec(memory_space=pltpu.VMEM)

    def exchange(rows):
        rows = rows.reshape(levels, lines, LANES)
        return lax.all_to_all(rows, "pairs", 0, 0, tiled=True).reshape(size, LANES)

    low = lax.dynamic_slice_in_dim(sector_mix, device, 1, 0)
    high = lax.dynamic_slice_in_dim(sector_mix, jnp.minimum(device + levels, 2 * levels - 2), 1, 0)
    mine = jnp.concatenate([low, high], 0)
    share = mine.shape[2]
    pieces = jnp.zeros((2, levels, LANES), jnp.float32)
    for step in range(col_devices):
        ring = [(i, (i + step) % col_devices) for i in range(col_devices)]
        part = lax.ppermute(mine, "cols", ring) if step else mine
        owner = (col_device - step) % col_devices
        pieces = lax.dynamic_update_slice(pieces, part, (0, 0, owner * share))

    packed = []
    for chunk in range(CHUNKS):
        packed.append(
            pl.pallas_call(
                pack_kernel,
                grid=(1,),
                in_specs=[pl.BlockSpec((2, levels, width), functools.partial(lambda c, i: (0, 0, c), chunk))],
                out_specs=pl.BlockSpec((size, LANES), lambda i: (0, 0)),
                out_shape=jax.ShapeDtypeStruct((size, LANES), jnp.float32),
                cost_estimate=pl.CostEstimate(flops=0, bytes_accessed=16 * levels * width, transcendentals=0),
                name="pack",
            )(state)
        )
    arrived = [exchange(p) for p in packed]

    n1 = device.astype(jnp.float32)
    n2 = jnp.arange(levels).astype(jnp.float32)
    phases = (kerr_rates[0] * n1 + kerr_rates[1] * n2)[:, None] * column_load.astype(jnp.float32)[None, :]
    cosine, sine = jnp.cos(phases), jnp.sin(phases)

    returned = []
    moments = []
    for chunk in range(CHUNKS):
        mixed, moment = pl.pallas_call(
            functools.partial(mix_kernel, chunk * width),
            in_specs=[vmem, vmem],
            out_specs=[vmem, vmem],
            out_shape=[
                jax.ShapeDtypeStruct((size, LANES), jnp.float32),
                jax.ShapeDtypeStruct((1, LANES), jnp.float32),
            ],
            cost_estimate=pl.CostEstimate(
                flops=12 * levels * size * LANES, bytes_accessed=16 * levels * width, transcendentals=0
            ),
            name="mix",
        )(arrived[chunk], pieces)
        moments.append(moment)
        returned.append(exchange(mixed))

    summed = lax.psum(jnp.sum(sum(moments)), ("pairs", "cols"))
    moment = summed / float(levels * levels * col_count * col_devices * levels * THIRD)

    evolved = None
    for chunk in range(CHUNKS):
        table = pl.BlockSpec((levels, width), functools.partial(lambda c, i: (0, c), chunk))
        inputs = [returned[chunk], cosine, sine]
        specs = [pl.BlockSpec((size, LANES), lambda i: (0, 0)), table, table]
        if chunk:
            inputs.append(evolved)
            specs.append(pl.BlockSpec(memory_space=pl.ANY))
        evolved = pl.pallas_call(
            functools.partial(turn_kernel, not chunk),
            grid=(1,),
            in_specs=specs,
            out_specs=pl.BlockSpec((2, levels, width), functools.partial(lambda c, i: (0, 0, c), chunk)),
            out_shape=jax.ShapeDtypeStruct((2, levels, col_count), jnp.float32),
            input_output_aliases={3: 0} if chunk else {},
            cost_estimate=pl.CostEstimate(flops=0, bytes_accessed=24 * levels * width, transcendentals=0),
            name="turn",
        )(*inputs)
    return evolved.reshape(2, 1, levels, col_count), moment.reshape(1)


def solution(mesh):
    placed = (P(None, "pairs", None, "cols"), P(None, None, "cols"), P(), P("cols"))
    return jax.shard_map(
        local,
        mesh=mesh,
        in_specs=placed,
        out_specs=(P(None, "pairs", None, "cols"), P()),
        check_vma=False,
    )
```

```python
import functools

import jax
import jax.numpy as jnp
from jax import lax
from jax.experimental import pallas as pl
from jax.experimental.pallas import tpu as pltpu
from jax.sharding import PartitionSpec as P

THIRD = 64
MEMB = 128
WINDOW = 2
LEVELS = 64
LANES = 128
STEPS = 4
VMEM_LIMIT = 24 * 1024 * 1024


def blend(low, high, shift):
    sub = lax.broadcasted_iota(jnp.int32, low.shape, 0)
    return jnp.where(sub < shift, low, high)


def pack_kernel(x_ref, out_ref):
    blocks = x_ref.shape[2] // LANES
    lines = 2 * blocks
    flat = out_ref.reshape(LEVELS * lines, LANES)
    n1 = lax.axis_index("pairs")
    tile, shift = n1 // 8, n1 % 8
    for part in range(2):
        for j in range(blocks):
            lanes = slice(j * LANES, (j + 1) * LANES)
            turned = [
                pltpu.roll(x_ref[part, 8 * a : 8 * a + 8, lanes], shift, 0) for a in range(LEVELS // 8)
            ]
            for a in range(LEVELS // 8):
                slot = 8 * ((a + tile) % 8)
                flat[pl.ds(slot * lines + part * blocks + j, 8, stride=lines), :] = blend(
                    turned[a - 1], turned[a], shift
                )


def split(values):
    high = values.astype(jnp.bfloat16)
    return high, (values - high.astype(jnp.float32)).astype(jnp.bfloat16)


def mix_kernel(col_count, x_ref, pieces_ref, out_ref, moment_ref, matrix_ref):
    lines = x_ref.shape[1]
    source = x_ref.reshape(LEVELS * lines, LANES)
    target = out_ref.reshape(LEVELS * lines, LANES)
    step = pl.program_id(0)
    row = lax.broadcasted_iota(jnp.int32, (LEVELS, LANES), 0)

    @pl.when(step == 0)
    def _():
        owner = lax.axis_index("pairs")
        col = lax.broadcasted_iota(jnp.int32, (LEVELS, LANES), 1)
        low = pieces_ref[0]
        high = pltpu.roll(pltpu.roll(pieces_ref[1], owner + 1, 0), owner + 1, 1)
        zero = jnp.zeros_like(low)
        low = jnp.where((row <= owner) & (col <= owner), low, zero)
        high = jnp.where((row > owner) & (col > owner) & (col < LEVELS), high, zero)
        top, rest = split((low + high)[:, :LEVELS])
        matrix_ref[...] = jnp.concatenate([top, top, rest], 1)
        moment_ref[...] = jnp.zeros_like(moment_ref)

    base = lax.axis_index("cols") * (col_count // (MEMB * WINDOW))
    total = jnp.zeros((LEVELS, LANES), jnp.float32)
    for line in range(0, lines, 2):
        top, rest = split(
            jnp.concatenate([source[pl.ds(line + i, LEVELS, stride=lines), :] for i in range(2)], 1)
        )
        mixed = jnp.dot(
            matrix_ref[...], jnp.concatenate([top, rest, top], 0), preferred_element_type=jnp.float32
        )
        for i in range(2):
            out = mixed[:, i * LANES : (i + 1) * LANES]
            target[pl.ds(line + i, LEVELS, stride=lines), :] = out
            column = ((step * lines + line + i) * LANES) % col_count
            third = base + column // (MEMB * WINDOW)
            total += (third + 1).astype(jnp.float32) * (out * out)
    moment_ref[...] += jnp.sum(total * (row + 1).astype(jnp.float32), axis=0, keepdims=True)


def turn_kernel(x_ref, cos_ref, sin_ref, out_ref):
    blocks = out_ref.shape[2] // LANES
    lines = 2 * blocks
    flat = x_ref.reshape(LEVELS * lines, LANES)
    n1 = lax.axis_index("pairs")
    tile, shift = n1 // 8, n1 % 8
    back = (8 - shift) % 8

    def rows(part, j):
        turned = []
        for a in range(LEVELS // 8):
            slot = 8 * ((a + tile) % 8)
            turned.append(
                pltpu.roll(flat[pl.ds(slot * lines + part * blocks + j, 8, stride=lines), :], back, 0)
            )
        return [blend(turned[a], turned[(a + 1) % 8], 8 - shift) for a in range(LEVELS // 8)]

    for j in range(blocks):
        lanes = slice(j * LANES, (j + 1) * LANES)
        real, imag = rows(0, j), rows(1, j)
        for a in range(LEVELS // 8):
            span = slice(8 * a, 8 * a + 8)
            cosine, sine = cos_ref[span, lanes], sin_ref[span, lanes]
            out_ref[0, span, lanes] = cosine * real[a] - sine * imag[a]
            out_ref[1, span, lanes] = sine * real[a] + cosine * imag[a]


def butterfly(value, axis):
    size = lax.axis_size(axis)
    reach = 1
    while reach < size:
        value = value + lax.ppermute(value, axis, [(i, i ^ reach) for i in range(size)])
        reach *= 2
    return value


def local(state, sector_mix, kerr_rates, column_load):
    pair_count = lax.axis_size("pairs")
    col_devices = lax.axis_size("cols")
    device = lax.axis_index("pairs")
    col_device = lax.axis_index("cols")
    levels, col_count = state.shape[2], state.shape[3]
    assert pair_count == levels == LEVELS and state.shape[1] == 1
    state = state.reshape(2, levels, col_count)
    blocks = col_count // LANES
    lines = 2 * blocks
    part = blocks // STEPS
    width = part * LANES
    params = pltpu.CompilerParams(vmem_limit_bytes=VMEM_LIMIT)

    def exchange(rows):
        return lax.all_to_all(rows, "pairs", 0, 0, tiled=True)

    low = lax.dynamic_slice_in_dim(sector_mix, device, 1, 0)
    high = lax.dynamic_slice_in_dim(sector_mix, jnp.minimum(device + levels, 2 * levels - 2), 1, 0)
    mine = jnp.concatenate([low, high], 0)
    share = mine.shape[2]
    pieces = jnp.zeros((2, levels, LANES), jnp.float32)
    for step in range(col_devices):
        ring = [(i, (i + step) % col_devices) for i in range(col_devices)]
        received = lax.ppermute(mine, "cols", ring) if step else mine
        owner = (col_device - step) % col_devices
        pieces = lax.dynamic_update_slice(pieces, received, (0, 0, owner * share))

    rows_spec = pl.BlockSpec((levels, 2, part, LANES), lambda i: (0, 0, i, 0))
    packed = pl.pallas_call(
        pack_kernel,
        grid=(STEPS,),
        in_specs=[pl.BlockSpec((2, levels, width), lambda i: (0, 0, i))],
        out_specs=rows_spec,
        out_shape=pltpu.HBM((levels, 2, blocks, LANES), jnp.float32),
        compiler_params=params,
        name="pack",
    )(pltpu.with_memory_space_constraint(state, pltpu.HBM))
    arrived = exchange(packed.reshape(levels, lines, LANES))

    n1 = device.astype(jnp.float32)
    n2 = jnp.arange(levels).astype(jnp.float32)
    phases = (kerr_rates[0] * n1 + kerr_rates[1] * n2)[:, None] * column_load.astype(jnp.float32)[None, :]
    cosine, sine = jnp.cos(phases), jnp.sin(phases)

    lines_spec = pl.BlockSpec((levels, lines // STEPS, LANES), lambda i: (0, i, 0))
    mixed, moment = pl.pallas_call(
        functools.partial(mix_kernel, col_count),
        grid=(STEPS,),
        in_specs=[lines_spec, pl.BlockSpec((2, levels, LANES), lambda i: (0, 0, 0))],
        out_specs=[lines_spec, pl.BlockSpec((1, LANES), lambda i: (0, 0))],
        out_shape=[
            pltpu.HBM((levels, lines, LANES), jnp.float32),
            jax.ShapeDtypeStruct((1, LANES), jnp.float32),
        ],
        scratch_shapes=[pltpu.VMEM((levels, 3 * levels), jnp.bfloat16)],
        compiler_params=params,
        name="mix",
    )(arrived, pieces)
    returned = exchange(mixed).reshape(levels, 2, blocks, LANES)

    summed = jnp.sum(butterfly(butterfly(moment, "cols"), "pairs"))
    moment = summed / float(levels * levels * col_count * col_devices * levels * THIRD)

    table = pl.BlockSpec((levels, width), lambda i: (0, i))
    evolved = pl.pallas_call(
        turn_kernel,
        grid=(STEPS,),
        in_specs=[rows_spec, table, table],
        out_specs=pl.BlockSpec((2, levels, width), lambda i: (0, 0, i)),
        out_shape=jax.ShapeDtypeStruct((2, levels, col_count), jnp.float32),
        compiler_params=params,
        name="turn",
    )(returned, cosine, sine)
    return evolved.reshape(2, 1, levels, col_count), moment.reshape(1)


def solution(mesh):
    placed = (P(None, "pairs", None, "cols"), P(None, None, "cols"), P(), P("cols"))
    return jax.shard_map(
        local,
        mesh=mesh,
        in_specs=placed,
        out_specs=(P(None, "pairs", None, "cols"), P()),
        check_vma=False,
    )
```

```python
import functools

import jax
import jax.numpy as jnp
from jax import lax
from jax.experimental import pallas as pl
from jax.experimental.pallas import tpu as pltpu
from jax.sharding import PartitionSpec as P

THIRD = 64
MEMB = 128
WINDOW = 2
LEVELS = 64
LANES = 128
STEPS = 4
VMEM_LIMIT = 24 * 1024 * 1024


def blend(low, high, shift):
    sub = lax.broadcasted_iota(jnp.int32, low.shape, 0)
    return jnp.where(sub < shift, low, high)


def pack_kernel(x_ref, out_ref):
    blocks = x_ref.shape[2] // LANES
    lines = 2 * blocks
    flat = out_ref.reshape(LEVELS * lines, LANES)
    n1 = lax.axis_index("pairs")
    tile, shift = n1 // 8, n1 % 8
    for part in range(2):
        for j in range(blocks):
            lanes = slice(j * LANES, (j + 1) * LANES)
            turned = [
                pltpu.roll(x_ref[part, 8 * a : 8 * a + 8, lanes], shift, 0) for a in range(LEVELS // 8)
            ]
            for a in range(LEVELS // 8):
                slot = 8 * ((a + tile) % 8)
                flat[pl.ds(slot * lines + part * blocks + j, 8, stride=lines), :] = blend(
                    turned[a - 1], turned[a], shift
                )


def split(values):
    high = values.astype(jnp.bfloat16)
    return high, (values - high.astype(jnp.float32)).astype(jnp.bfloat16)


def mix_kernel(col_count, x_ref, pieces_ref, out_ref, moment_ref, matrix_ref):
    lines = x_ref.shape[1]
    source = x_ref.reshape(LEVELS * lines, LANES)
    target = out_ref.reshape(LEVELS * lines, LANES)
    step = pl.program_id(0)
    row = lax.broadcasted_iota(jnp.int32, (LEVELS, LANES), 0)

    @pl.when(step == 0)
    def _():
        owner = lax.axis_index("pairs")
        col = lax.broadcasted_iota(jnp.int32, (LEVELS, LANES), 1)
        low = pieces_ref[0]
        high = pltpu.roll(pltpu.roll(pieces_ref[1], owner + 1, 0), owner + 1, 1)
        zero = jnp.zeros_like(low)
        low = jnp.where((row <= owner) & (col <= owner), low, zero)
        high = jnp.where((row > owner) & (col > owner) & (col < LEVELS), high, zero)
        top, rest = split((low + high)[:, :LEVELS])
        matrix_ref[...] = jnp.concatenate([top, top, rest], 1)
        moment_ref[...] = jnp.zeros_like(moment_ref)

    base = lax.axis_index("cols") * (col_count // (MEMB * WINDOW))
    total = jnp.zeros((LEVELS, LANES), jnp.float32)
    for line in range(0, lines, 2):
        top, rest = split(
            jnp.concatenate([source[pl.ds(line + i, LEVELS, stride=lines), :] for i in range(2)], 1)
        )
        mixed = jnp.dot(
            matrix_ref[...], jnp.concatenate([top, rest, top], 0), preferred_element_type=jnp.float32
        )
        for i in range(2):
            out = mixed[:, i * LANES : (i + 1) * LANES]
            target[pl.ds(line + i, LEVELS, stride=lines), :] = out
            column = (step * (lines // 2) + (line + i) % (lines // 2)) * LANES
            third = base + column // (MEMB * WINDOW)
            total += (third + 1).astype(jnp.float32) * (out * out)
    moment_ref[...] += jnp.sum(total * (row + 1).astype(jnp.float32), axis=0, keepdims=True)


def turn_kernel(x_ref, cos_ref, sin_ref, out_ref):
    blocks = out_ref.shape[2] // LANES
    lines = 2 * blocks
    flat = x_ref.reshape(LEVELS * lines, LANES)
    n1 = lax.axis_index("pairs")
    tile, shift = n1 // 8, n1 % 8
    back = (8 - shift) % 8

    def rows(part, j):
        turned = []
        for a in range(LEVELS // 8):
            slot = 8 * ((a + tile) % 8)
            turned.append(
                pltpu.roll(flat[pl.ds(slot * lines + part * blocks + j, 8, stride=lines), :], back, 0)
            )
        return [blend(turned[a], turned[(a + 1) % 8], 8 - shift) for a in range(LEVELS // 8)]

    for j in range(blocks):
        lanes = slice(j * LANES, (j + 1) * LANES)
        real, imag = rows(0, j), rows(1, j)
        for a in range(LEVELS // 8):
            span = slice(8 * a, 8 * a + 8)
            cosine, sine = cos_ref[span, lanes], sin_ref[span, lanes]
            out_ref[0, span, lanes] = cosine * real[a] - sine * imag[a]
            out_ref[1, span, lanes] = sine * real[a] + cosine * imag[a]


def butterfly(value, axis):
    size = lax.axis_size(axis)
    reach = 1
    while reach < size:
        value = value + lax.ppermute(value, axis, [(i, i ^ reach) for i in range(size)])
        reach *= 2
    return value


def local(state, sector_mix, kerr_rates, column_load):
    pair_count = lax.axis_size("pairs")
    col_devices = lax.axis_size("cols")
    device = lax.axis_index("pairs")
    col_device = lax.axis_index("cols")
    levels, col_count = state.shape[2], state.shape[3]
    assert pair_count == levels == LEVELS and state.shape[1] == 1
    state = state.reshape(2, levels, col_count)
    blocks = col_count // LANES
    lines = 2 * blocks
    part = blocks // STEPS
    width = part * LANES
    params = pltpu.CompilerParams(vmem_limit_bytes=VMEM_LIMIT)

    def exchange(rows):
        return lax.all_to_all(rows, "pairs", 0, 0, tiled=True)

    low = lax.dynamic_slice_in_dim(sector_mix, device, 1, 0)
    high = lax.dynamic_slice_in_dim(sector_mix, jnp.minimum(device + levels, 2 * levels - 2), 1, 0)
    mine = jnp.concatenate([low, high], 0)
    share = mine.shape[2]
    pieces = jnp.zeros((2, levels, LANES), jnp.float32)
    for step in range(col_devices):
        ring = [(i, (i + step) % col_devices) for i in range(col_devices)]
        received = lax.ppermute(mine, "cols", ring) if step else mine
        owner = (col_device - step) % col_devices
        pieces = lax.dynamic_update_slice(pieces, received, (0, 0, owner * share))

    rows_spec = pl.BlockSpec((levels, 2 * part, LANES), lambda i: (0, i, 0))
    packed = pl.pallas_call(
        pack_kernel,
        grid=(STEPS,),
        in_specs=[pl.BlockSpec((2, levels, width), lambda i: (0, 0, i))],
        out_specs=rows_spec,
        out_shape=pltpu.HBM((levels, lines, LANES), jnp.float32),
        compiler_params=params,
        name="pack",
    )(pltpu.with_memory_space_constraint(state, pltpu.HBM))
    arrived = exchange(packed)

    n1 = device.astype(jnp.float32)
    n2 = jnp.arange(levels).astype(jnp.float32)
    phases = (kerr_rates[0] * n1 + kerr_rates[1] * n2)[:, None] * column_load.astype(jnp.float32)[None, :]
    cosine, sine = jnp.cos(phases), jnp.sin(phases)

    arrived, cosine, sine = lax.optimization_barrier((arrived, cosine, sine))
    mixed, moment = pl.pallas_call(
        functools.partial(mix_kernel, col_count),
        grid=(STEPS,),
        in_specs=[rows_spec, pl.BlockSpec((2, levels, LANES), lambda i: (0, 0, 0))],
        out_specs=[rows_spec, pl.BlockSpec((1, LANES), lambda i: (0, 0))],
        out_shape=[
            pltpu.HBM((levels, lines, LANES), jnp.float32),
            jax.ShapeDtypeStruct((1, LANES), jnp.float32),
        ],
        scratch_shapes=[pltpu.VMEM((levels, 3 * levels), jnp.bfloat16)],
        compiler_params=params,
        name="mix",
    )(arrived, pieces)
    returned = exchange(mixed)

    summed = jnp.sum(butterfly(butterfly(moment, "cols"), "pairs"))
    moment = summed / float(levels * levels * col_count * col_devices * levels * THIRD)

    table = pl.BlockSpec((levels, width), lambda i: (0, i))
    evolved = pl.pallas_call(
        turn_kernel,
        grid=(STEPS,),
        in_specs=[rows_spec, table, table],
        out_specs=pl.BlockSpec((2, levels, width), lambda i: (0, 0, i)),
        out_shape=jax.ShapeDtypeStruct((2, levels, col_count), jnp.float32),
        compiler_params=params,
        name="turn",
    )(returned, *(pltpu.with_memory_space_constraint(t, pltpu.HBM) for t in (cosine, sine)))
    return evolved.reshape(2, 1, levels, col_count), moment.reshape(1)


def solution(mesh):
    placed = (P(None, "pairs", None, "cols"), P(None, None, "cols"), P(), P("cols"))
    return jax.shard_map(
        local,
        mesh=mesh,
        in_specs=placed,
        out_specs=(P(None, "pairs", None, "cols"), P()),
        check_vma=False,
    )
```

```python
import functools

import jax
import jax.numpy as jnp
from jax import lax
from jax.experimental import pallas as pl
from jax.experimental.pallas import tpu as pltpu
from jax.sharding import PartitionSpec as P

THIRD = 64
MEMB = 128
WINDOW = 2
LEVELS = 64
LANES = 128
STEPS = 4
VMEM_LIMIT = 24 * 1024 * 1024


def blend(low, high, shift):
    sub = lax.broadcasted_iota(jnp.int32, low.shape, 0)
    return jnp.where(sub < shift, low, high)


def pack_kernel(x_ref, out_ref, x_buf, out_buf, in_sem, out_sem):
    steps, lines = out_buf.shape[0], out_buf.shape[1] // LEVELS
    blocks = lines // 2
    width = blocks * LANES
    n1 = lax.axis_index("pairs")
    tile, shift = n1 // 8, n1 % 8
    loads = [
        pltpu.make_async_copy(x_ref.at[:, :, pl.ds(k * width, width)], x_buf.at[k], in_sem.at[k])
        for k in range(steps)
    ]
    stores = [
        pltpu.make_async_copy(
            out_buf.at[k].reshape(LEVELS, lines, LANES), out_ref.at[:, pl.ds(k * lines, lines), :], out_sem.at[k]
        )
        for k in range(steps)
    ]
    for load in loads:
        load.start()
    for k in range(steps):
        loads[k].wait()
        for part in range(2):
            for j in range(blocks):
                lanes = slice(j * LANES, (j + 1) * LANES)
                turned = [
                    pltpu.roll(x_buf[k, part, 8 * a : 8 * a + 8, lanes], shift, 0) for a in range(LEVELS // 8)
                ]
                for a in range(LEVELS // 8):
                    slot = 8 * ((a + tile) % 8)
                    out_buf[k, pl.ds(slot * lines + part * blocks + j, 8, stride=lines), :] = blend(
                        turned[a - 1], turned[a], shift
                    )
        stores[k].start()
    for store in stores:
        store.wait()


def split(values):
    high = values.astype(jnp.bfloat16)
    return high, (values - high.astype(jnp.float32)).astype(jnp.bfloat16)


def mix_kernel(col_count, x_ref, pieces_ref, out_ref, moment_ref, out_buf, out_sem):
    steps, lines = out_buf.shape[0], out_buf.shape[1] // LEVELS
    blocks = lines // 2
    pitch = steps * lines
    source = x_ref.reshape(LEVELS * pitch, LANES)
    stores = [
        pltpu.make_async_copy(
            out_buf.at[k].reshape(LEVELS, lines, LANES), out_ref.at[:, pl.ds(k * lines, lines), :], out_sem.at[k]
        )
        for k in range(steps)
    ]
    owner = lax.axis_index("pairs")
    base = lax.axis_index("cols") * (col_count // (MEMB * WINDOW))
    row = lax.broadcasted_iota(jnp.int32, (LEVELS, LANES), 0)
    col = lax.broadcasted_iota(jnp.int32, (LEVELS, LANES), 1)
    low = pieces_ref[0]
    high = pltpu.roll(pltpu.roll(pieces_ref[1], owner + 1, 0), owner + 1, 1)
    zero = jnp.zeros_like(low)
    low = jnp.where((row <= owner) & (col <= owner), low, zero)
    high = jnp.where((row > owner) & (col > owner) & (col < LEVELS), high, zero)
    top, rest = split((low + high)[:, :LEVELS])
    matrix = jnp.concatenate([top, top, rest], 1)
    total = jnp.zeros((LEVELS, LANES), jnp.float32)
    for k in range(steps):
        for line in range(0, lines, 2):
            top, rest = split(
                jnp.concatenate([source[pl.ds(k * lines + line + i, LEVELS, stride=pitch), :] for i in range(2)], 1)
            )
            mixed = jnp.dot(matrix, jnp.concatenate([top, rest, top], 0), preferred_element_type=jnp.float32)
            for i in range(2):
                out = mixed[:, i * LANES : (i + 1) * LANES]
                out_buf[k, pl.ds(line + i, LEVELS, stride=lines), :] = out
                third = base + (k * blocks + (line + i) % blocks) * LANES // (MEMB * WINDOW)
                total += (third + 1).astype(jnp.float32) * (out * out)
        stores[k].start()
    moment_ref[...] = jnp.sum(total * (row + 1).astype(jnp.float32), axis=0, keepdims=True)
    for store in stores:
        store.wait()


def turn_kernel(x_ref, cos_tile_ref, sin_tile_ref, cos_row_ref, sin_row_ref, out_ref, out_buf, out_sem):
    steps, width = out_buf.shape[0], out_buf.shape[3]
    blocks = width // LANES
    lines = 2 * blocks
    pitch = steps * lines
    flat = x_ref.reshape(LEVELS * pitch, LANES)
    n1 = lax.axis_index("pairs")
    tile, shift = n1 // 8, n1 % 8
    back = (8 - shift) % 8
    stores = [
        pltpu.make_async_copy(out_buf.at[k], out_ref.at[:, :, pl.ds(k * width, width)], out_sem.at[k])
        for k in range(steps)
    ]

    def rows(line):
        turned = []
        for a in range(LEVELS // 8):
            slot = 8 * ((a + tile) % 8)
            turned.append(pltpu.roll(flat[pl.ds(slot * pitch + line, 8, stride=pitch), :], back, 0))
        return [blend(turned[a], turned[(a + 1) % 8], 8 - shift) for a in range(LEVELS // 8)]

    for k in range(steps):
        for j in range(blocks):
            lanes = slice(j * LANES, (j + 1) * LANES)
            wide = slice(k * width + j * LANES, k * width + (j + 1) * LANES)
            real, imag = rows(k * lines + j), rows(k * lines + blocks + j)
            cos_row, sin_row = cos_row_ref[:, wide], sin_row_ref[:, wide]
            for a in range(LEVELS // 8):
                span = slice(8 * a, 8 * a + 8)
                cos_tile = cos_tile_ref[a : a + 1, wide]
                sin_tile = sin_tile_ref[a : a + 1, wide]
                cosine = cos_tile * cos_row - sin_tile * sin_row
                sine = sin_tile * cos_row + cos_tile * sin_row
                out_buf[k, 0, span, lanes] = cosine * real[a] - sine * imag[a]
                out_buf[k, 1, span, lanes] = sine * real[a] + cosine * imag[a]
        stores[k].start()
    for store in stores:
        store.wait()


def butterfly(value, axis, last):
    size = lax.axis_size(axis)

    def partner(reach):
        return lax.ppermute(value, axis, [(i, i ^ reach) for i in range(size)])

    reach = 1
    while reach < size // last:
        value = value + partner(reach)
        reach *= 2
    terms = [value] + [partner(reach * i) for i in range(1, last)]
    while len(terms) > 1:
        terms = [terms[i] + terms[i + 1] for i in range(0, len(terms), 2)]
    return terms[0]


def local(state, sector_mix, kerr_rates, column_load):
    pair_count = lax.axis_size("pairs")
    col_devices = lax.axis_size("cols")
    device = lax.axis_index("pairs")
    col_device = lax.axis_index("cols")
    levels, col_count = state.shape[2], state.shape[3]
    assert pair_count == levels == LEVELS and state.shape[1] == 1
    state = state.reshape(2, levels, col_count)
    blocks = col_count // LANES
    lines = 2 * blocks
    part = blocks // STEPS
    width = part * LANES
    params = pltpu.CompilerParams(vmem_limit_bytes=VMEM_LIMIT)

    def exchange(rows):
        return lax.all_to_all(rows, "pairs", 0, 0, tiled=True)

    low = lax.dynamic_slice_in_dim(sector_mix, device, 1, 0)
    high = lax.dynamic_slice_in_dim(sector_mix, jnp.minimum(device + levels, 2 * levels - 2), 1, 0)
    mine = jnp.concatenate([low, high], 0)
    share = mine.shape[2]
    pieces = jnp.zeros((2, levels, LANES), jnp.float32)
    for step in range(col_devices):
        ring = [(i, (i + step) % col_devices) for i in range(col_devices)]
        received = lax.ppermute(mine, "cols", ring) if step else mine
        owner = (col_device - step) % col_devices
        pieces = lax.dynamic_update_slice(pieces, received, (0, 0, owner * share))

    anywhere = pl.BlockSpec(memory_space=pl.ANY)
    vmem = pl.BlockSpec(memory_space=pltpu.VMEM)
    rows_shape = pltpu.HBM((levels, lines, LANES), jnp.float32)
    rows_buf = pltpu.VMEM((STEPS, levels * 2 * part, LANES), jnp.float32)
    state_buf = pltpu.VMEM((STEPS, 2, levels, width), jnp.float32)
    sems = pltpu.SemaphoreType.DMA((STEPS,))

    packed = pl.pallas_call(
        pack_kernel,
        in_specs=[anywhere],
        out_specs=anywhere,
        out_shape=rows_shape,
        scratch_shapes=[state_buf, rows_buf, sems, sems],
        compiler_params=params,
        name="pack",
    )(pltpu.with_memory_space_constraint(state, pltpu.HBM))
    arrived = exchange(packed)

    n1 = device.astype(jnp.float32)
    eight = jnp.arange(8).astype(jnp.float32)
    loads = column_load.astype(jnp.float32)[None, :]
    tile_phases = (kerr_rates[0] * n1 + kerr_rates[1] * (8.0 * eight))[:, None] * loads
    row_phases = (kerr_rates[1] * eight)[:, None] * loads
    tables = (jnp.cos(tile_phases), jnp.sin(tile_phases), jnp.cos(row_phases), jnp.sin(row_phases))
    arrived, tables = lax.optimization_barrier((arrived, tables))

    mixed, moment = pl.pallas_call(
        functools.partial(mix_kernel, col_count),
        in_specs=[vmem, vmem],
        out_specs=[anywhere, vmem],
        out_shape=[rows_shape, jax.ShapeDtypeStruct((1, LANES), jnp.float32)],
        scratch_shapes=[rows_buf, sems],
        compiler_params=params,
        name="mix",
    )(arrived, pieces)
    returned = exchange(mixed)

    summed = jnp.sum(butterfly(butterfly(moment, "cols", 2), "pairs", 8))
    moment = summed / float(levels * levels * col_count * col_devices * levels * THIRD)

    evolved = pl.pallas_call(
        turn_kernel,
        in_specs=[vmem] * 5,
        out_specs=anywhere,
        out_shape=pltpu.HBM((2, levels, col_count), jnp.float32),
        scratch_shapes=[state_buf, sems],
        compiler_params=params,
        name="turn",
    )(returned, *tables)
    return evolved.reshape(2, 1, levels, col_count), moment.reshape(1)


def solution(mesh):
    placed = (P(None, "pairs", None, "cols"), P(None, None, "cols"), P(), P("cols"))
    return jax.shard_map(
        local,
        mesh=mesh,
        in_specs=placed,
        out_specs=(P(None, "pairs", None, "cols"), P()),
        check_vma=False,
    )
```

```python
import functools

import jax
import jax.numpy as jnp
from jax import lax
from jax.experimental import pallas as pl
from jax.experimental.pallas import tpu as pltpu
from jax.sharding import PartitionSpec as P

THIRD = 64
MEMB = 128
WINDOW = 2
LEVELS = 64
LANES = 128
STEPS = 8
VMEM_LIMIT = 24 * 1024 * 1024


def blend(low, high, shift):
    sub = lax.broadcasted_iota(jnp.int32, low.shape, 0)
    return jnp.where(sub < shift, low, high)


def pack_kernel(x_ref, out_ref, x_buf, out_buf, in_sem, out_sem):
    steps, lines = out_buf.shape[0], out_buf.shape[1] // LEVELS
    blocks = lines // 2
    width = blocks * LANES
    n1 = lax.axis_index("pairs")
    tile, shift = n1 // 8, n1 % 8
    loads = [
        pltpu.make_async_copy(x_ref.at[:, :, pl.ds(k * width, width)], x_buf.at[k], in_sem.at[k])
        for k in range(steps)
    ]
    stores = [
        pltpu.make_async_copy(
            out_buf.at[k].reshape(LEVELS, lines, LANES), out_ref.at[:, pl.ds(k * lines, lines), :], out_sem.at[k]
        )
        for k in range(steps)
    ]
    for load in loads:
        load.start()
    for k in range(steps):
        loads[k].wait()
        for part in range(2):
            for j in range(blocks):
                lanes = slice(j * LANES, (j + 1) * LANES)
                turned = [
                    pltpu.roll(x_buf[k, part, 8 * a : 8 * a + 8, lanes], shift, 0) for a in range(LEVELS // 8)
                ]
                for a in range(LEVELS // 8):
                    slot = 8 * ((a + tile) % 8)
                    out_buf[k, pl.ds(slot * lines + part * blocks + j, 8, stride=lines), :] = blend(
                        turned[a - 1], turned[a], shift
                    )
        stores[k].start()
    for store in stores:
        store.wait()


def split(values):
    high = values.astype(jnp.bfloat16)
    return high, (values - high.astype(jnp.float32)).astype(jnp.bfloat16)


def matrix_kernel(pieces_ref, matrix_ref):
    owner = lax.axis_index("pairs")
    row = lax.broadcasted_iota(jnp.int32, (LEVELS, LANES), 0)
    col = lax.broadcasted_iota(jnp.int32, (LEVELS, LANES), 1)
    low = pieces_ref[0]
    high = pltpu.roll(pltpu.roll(pieces_ref[1], owner + 1, 0), owner + 1, 1)
    zero = jnp.zeros_like(low)
    low = jnp.where((row <= owner) & (col <= owner), low, zero)
    high = jnp.where((row > owner) & (col > owner) & (col < LEVELS), high, zero)
    top, rest = split((low + high)[:, :LEVELS])
    matrix_ref[...] = jnp.concatenate([top, top, rest], 1)


def mix_kernel(col_count, x_ref, matrix_ref, out_ref, moment_ref, out_buf, out_sem):
    steps, lines = out_buf.shape[0], out_buf.shape[1] // LEVELS
    blocks = lines // 2
    pitch = steps * lines
    source = x_ref.reshape(LEVELS * pitch, LANES)
    stores = [
        pltpu.make_async_copy(
            out_buf.at[k].reshape(LEVELS, lines, LANES), out_ref.at[:, pl.ds(k * lines, lines), :], out_sem.at[k]
        )
        for k in range(steps)
    ]
    base = lax.axis_index("cols") * (col_count // (MEMB * WINDOW))
    row = lax.broadcasted_iota(jnp.int32, (LEVELS, LANES), 0)
    matrix = matrix_ref[...]
    total = jnp.zeros((LEVELS, LANES), jnp.float32)
    for k in range(steps):
        for line in range(0, lines, 2):
            top, rest = split(
                jnp.concatenate([source[pl.ds(k * lines + line + i, LEVELS, stride=pitch), :] for i in range(2)], 1)
            )
            mixed = jnp.dot(matrix, jnp.concatenate([top, rest, top], 0), preferred_element_type=jnp.float32)
            for i in range(2):
                out = mixed[:, i * LANES : (i + 1) * LANES]
                out_buf[k, pl.ds(line + i, LEVELS, stride=lines), :] = out
                third = base + (k * blocks + (line + i) % blocks) * LANES // (MEMB * WINDOW)
                total += (third + 1).astype(jnp.float32) * (out * out)
        stores[k].start()
    moment_ref[...] = jnp.sum(total * (row + 1).astype(jnp.float32), axis=0, keepdims=True)
    for store in stores:
        store.wait()


def turn_kernel(total, x_ref, cos_tile_ref, sin_tile_ref, cos_row_ref, sin_row_ref, *refs):
    *term_refs, out_ref, moment_ref, out_buf, moment_buf, out_sem, moment_sem = refs
    moment = pltpu.make_async_copy(moment_buf, moment_ref, moment_sem)
    steps, width = out_buf.shape[0], out_buf.shape[3]
    blocks = width // LANES
    lines = 2 * blocks
    pitch = steps * lines
    flat = x_ref.reshape(LEVELS * pitch, LANES)
    n1 = lax.axis_index("pairs")
    tile, shift = n1 // 8, n1 % 8
    back = (8 - shift) % 8
    stores = [
        pltpu.make_async_copy(out_buf.at[k], out_ref.at[:, :, pl.ds(k * width, width)], out_sem.at[k])
        for k in range(steps)
    ]

    def rows(line):
        turned = []
        for a in range(LEVELS // 8):
            slot = 8 * ((a + tile) % 8)
            turned.append(pltpu.roll(flat[pl.ds(slot * pitch + line, 8, stride=pitch), :], back, 0))
        return [blend(turned[a], turned[(a + 1) % 8], 8 - shift) for a in range(LEVELS // 8)]

    for k in range(steps):
        for j in range(blocks):
            lanes = slice(j * LANES, (j + 1) * LANES)
            wide = slice(k * width + j * LANES, k * width + (j + 1) * LANES)
            real, imag = rows(k * lines + j), rows(k * lines + blocks + j)
            cos_row, sin_row = cos_row_ref[:, wide], sin_row_ref[:, wide]
            for a in range(LEVELS // 8):
                span = slice(8 * a, 8 * a + 8)
                cos_tile = cos_tile_ref[a : a + 1, wide]
                sin_tile = sin_tile_ref[a : a + 1, wide]
                cosine = cos_tile * cos_row - sin_tile * sin_row
                sine = sin_tile * cos_row + cos_tile * sin_row
                out_buf[k, 0, span, lanes] = cosine * real[a] - sine * imag[a]
                out_buf[k, 1, span, lanes] = sine * real[a] + cosine * imag[a]
        stores[k].start()
        if k == 0:
            moment_buf[0] = jnp.sum(tree([term[...] for term in term_refs])) / total
            moment.start()
    moment.wait()
    for store in stores:
        store.wait()


def butterfly(value, axis, last):
    size = lax.axis_size(axis)

    def partner(reach):
        return lax.ppermute(value, axis, [(i, i ^ reach) for i in range(size)])

    reach = 1
    while reach < size // last:
        value = value + partner(reach)
        reach *= 2
    return [value] + [partner(reach * i) for i in range(1, last)]


def tree(terms):
    while len(terms) > 1:
        terms = [terms[i] + terms[i + 1] for i in range(0, len(terms), 2)]
    return terms[0]


def local(state, sector_mix, kerr_rates, column_load):
    pair_count = lax.axis_size("pairs")
    col_devices = lax.axis_size("cols")
    device = lax.axis_index("pairs")
    col_device = lax.axis_index("cols")
    levels, col_count = state.shape[2], state.shape[3]
    assert pair_count == levels == LEVELS and state.shape[1] == 1
    state = state.reshape(2, levels, col_count)
    blocks = col_count // LANES
    lines = 2 * blocks
    part = blocks // STEPS
    width = part * LANES
    params = pltpu.CompilerParams(vmem_limit_bytes=VMEM_LIMIT)

    def exchange(rows):
        return lax.all_to_all(rows, "pairs", 0, 0, tiled=True)

    low = lax.dynamic_slice_in_dim(sector_mix, device, 1, 0)
    high = lax.dynamic_slice_in_dim(sector_mix, jnp.minimum(device + levels, 2 * levels - 2), 1, 0)
    mine = jnp.concatenate([low, high], 0)
    share = mine.shape[2]
    pieces = jnp.zeros((2, levels, LANES), jnp.float32)
    for step in range(col_devices):
        ring = [(i, (i + step) % col_devices) for i in range(col_devices)]
        received = lax.ppermute(mine, "cols", ring) if step else mine
        owner = (col_device - step) % col_devices
        pieces = lax.dynamic_update_slice(pieces, received, (0, 0, owner * share))

    anywhere = pl.BlockSpec(memory_space=pl.ANY)
    vmem = pl.BlockSpec(memory_space=pltpu.VMEM)
    rows_shape = pltpu.HBM((levels, lines, LANES), jnp.float32)
    rows_buf = pltpu.VMEM((STEPS, levels * 2 * part, LANES), jnp.float32)
    state_buf = pltpu.VMEM((STEPS, 2, levels, width), jnp.float32)
    sems = pltpu.SemaphoreType.DMA((STEPS,))

    packed = pl.pallas_call(
        pack_kernel,
        in_specs=[anywhere],
        out_specs=anywhere,
        out_shape=rows_shape,
        scratch_shapes=[state_buf, rows_buf, sems, sems],
        compiler_params=params,
        name="pack",
    )(pltpu.with_memory_space_constraint(state, pltpu.HBM))
    arrived = exchange(packed)

    n1 = device.astype(jnp.float32)
    eight = jnp.arange(8).astype(jnp.float32)
    loads = column_load.astype(jnp.float32)[None, :]
    tile_phases = (kerr_rates[0] * n1 + kerr_rates[1] * (8.0 * eight))[:, None] * loads
    row_phases = (kerr_rates[1] * eight)[:, None] * loads
    tables = (jnp.cos(tile_phases), jnp.sin(tile_phases), jnp.cos(row_phases), jnp.sin(row_phases))
    matrix = pl.pallas_call(
        matrix_kernel,
        in_specs=[vmem],
        out_specs=vmem,
        out_shape=jax.ShapeDtypeStruct((levels, 3 * levels), jnp.bfloat16),
        compiler_params=params,
        name="matrix",
    )(pieces)
    arrived, tables, matrix = lax.optimization_barrier((arrived, tables, matrix))

    mixed, moment = pl.pallas_call(
        functools.partial(mix_kernel, col_count),
        in_specs=[vmem, vmem],
        out_specs=[anywhere, vmem],
        out_shape=[rows_shape, jax.ShapeDtypeStruct((1, LANES), jnp.float32)],
        scratch_shapes=[rows_buf, sems],
        compiler_params=params,
        name="mix",
    )(arrived, matrix)
    returned = exchange(mixed)

    terms = butterfly(tree(butterfly(moment, "cols", 2)), "pairs", 8)
    total = float(levels * levels * col_count * col_devices * levels * THIRD)

    evolved, moment = pl.pallas_call(
        functools.partial(turn_kernel, total),
        in_specs=[vmem] * (5 + len(terms)),
        out_specs=[anywhere, anywhere],
        out_shape=[pltpu.HBM((2, levels, col_count), jnp.float32), pltpu.HBM((1,), jnp.float32)],
        scratch_shapes=[state_buf, pltpu.SMEM((1,), jnp.float32), sems, pltpu.SemaphoreType.DMA],
        compiler_params=params,
        name="turn",
    )(returned, *tables, *terms)
    return evolved.reshape(2, 1, levels, col_count), moment


def solution(mesh):
    placed = (P(None, "pairs", None, "cols"), P(None, None, "cols"), P(), P("cols"))
    return jax.shard_map(
        local,
        mesh=mesh,
        in_specs=placed,
        out_specs=(P(None, "pairs", None, "cols"), P()),
        check_vma=False,
    )
```

```python
import functools

import jax
import jax.numpy as jnp
from jax import lax
from jax.experimental import pallas as pl
from jax.experimental.pallas import tpu as pltpu
from jax.sharding import PartitionSpec as P

THIRD = 64
MEMB = 128
WINDOW = 2
LEVELS = 64
LANES = 128
STEPS = 8
VMEM_LIMIT = 24 * 1024 * 1024


def blend(low, high, shift):
    sub = lax.broadcasted_iota(jnp.int32, low.shape, 0)
    return jnp.where(sub < shift, low, high)


def pack_kernel(x_ref, out_ref, x_buf, out_buf, in_sem, out_sem):
    steps, lines = out_buf.shape[0], out_buf.shape[1] // LEVELS
    blocks = lines // 2
    width = blocks * LANES
    n1 = lax.axis_index("pairs")
    tile, shift = n1 // 8, n1 % 8
    loads = [
        pltpu.make_async_copy(x_ref.at[:, :, pl.ds(k * width, width)], x_buf.at[k], in_sem.at[k])
        for k in range(steps)
    ]
    stores = [
        pltpu.make_async_copy(
            out_buf.at[k].reshape(LEVELS, lines, LANES), out_ref.at[:, pl.ds(k * lines, lines), :], out_sem.at[k]
        )
        for k in range(steps)
    ]
    for load in loads:
        load.start()
    for k in range(steps):
        loads[k].wait()
        for part in range(2):
            for j in range(blocks):
                lanes = slice(j * LANES, (j + 1) * LANES)
                turned = [
                    pltpu.roll(x_buf[k, part, 8 * a : 8 * a + 8, lanes], shift, 0) for a in range(LEVELS // 8)
                ]
                for a in range(LEVELS // 8):
                    slot = 8 * ((a + tile) % 8)
                    out_buf[k, pl.ds(slot * lines + part * blocks + j, 8, stride=lines), :] = blend(
                        turned[a - 1], turned[a], shift
                    )
        stores[k].start()
    for store in stores:
        store.wait()


def split(values):
    high = values.astype(jnp.bfloat16)
    return high, (values - high.astype(jnp.float32)).astype(jnp.bfloat16)


def matrix_kernel(pieces_ref, matrix_ref):
    owner = lax.axis_index("pairs")
    row = lax.broadcasted_iota(jnp.int32, (LEVELS, LANES), 0)
    col = lax.broadcasted_iota(jnp.int32, (LEVELS, LANES), 1)
    low = pieces_ref[0]
    high = pltpu.roll(pltpu.roll(pieces_ref[1], owner + 1, 0), owner + 1, 1)
    zero = jnp.zeros_like(low)
    low = jnp.where((row <= owner) & (col <= owner), low, zero)
    high = jnp.where((row > owner) & (col > owner) & (col < LEVELS), high, zero)
    top, rest = split((low + high)[:, :LEVELS])
    matrix_ref[...] = jnp.concatenate([top, top, rest], 1)


def mix_kernel(col_count, x_ref, matrix_ref, out_ref, moment_ref, out_buf, out_sem):
    steps, lines = out_buf.shape[0], out_buf.shape[1] // LEVELS
    blocks = lines // 2
    pitch = steps * lines
    source = x_ref.reshape(LEVELS * pitch, LANES)
    stores = [
        pltpu.make_async_copy(
            out_buf.at[k].reshape(LEVELS, lines, LANES), out_ref.at[:, pl.ds(k * lines, lines), :], out_sem.at[k]
        )
        for k in range(steps)
    ]
    base = lax.axis_index("cols") * (col_count // (MEMB * WINDOW))
    matrix = matrix_ref[...]
    for k in range(steps):
        for line in range(0, lines, 2):
            top, rest = split(
                jnp.concatenate([source[pl.ds(k * lines + line + i, LEVELS, stride=pitch), :] for i in range(2)], 1)
            )
            mixed = jnp.dot(matrix, jnp.concatenate([top, rest, top], 0), preferred_element_type=jnp.float32)
            for i in range(2):
                out = mixed[:, i * LANES : (i + 1) * LANES]
                out_buf[k, pl.ds(line + i, LEVELS, stride=lines), :] = out
        stores[k].start()
    line = lax.broadcasted_iota(jnp.int32, (lines, LANES), 0)
    total = jnp.zeros((lines, LANES), jnp.float32)
    for k in range(steps):
        part = jnp.zeros((lines, LANES), jnp.float32)
        for n1 in range(LEVELS):
            out = out_buf[k, n1 * lines : (n1 + 1) * lines, :]
            part += float(n1 + 1) * (out * out)
        third = base + (k * blocks + line % blocks) * LANES // (MEMB * WINDOW)
        total += (third + 1).astype(jnp.float32) * part
    moment_ref[...] = jnp.sum(total, axis=0, keepdims=True)
    for store in stores:
        store.wait()


def turn_kernel(total, x_ref, cos_tile_ref, sin_tile_ref, cos_row_ref, sin_row_ref, *refs):
    *term_refs, out_ref, moment_ref, out_buf, moment_buf, out_sem, moment_sem = refs
    moment = pltpu.make_async_copy(moment_buf, moment_ref, moment_sem)
    steps, width = out_buf.shape[0], out_buf.shape[3]
    blocks = width // LANES
    lines = 2 * blocks
    pitch = steps * lines
    flat = x_ref.reshape(LEVELS * pitch, LANES)
    n1 = lax.axis_index("pairs")
    tile, shift = n1 // 8, n1 % 8
    back = (8 - shift) % 8
    stores = [
        pltpu.make_async_copy(out_buf.at[k], out_ref.at[:, :, pl.ds(k * width, width)], out_sem.at[k])
        for k in range(steps)
    ]

    def rows(line):
        turned = []
        for a in range(LEVELS // 8):
            slot = 8 * ((a + tile) % 8)
            turned.append(pltpu.roll(flat[pl.ds(slot * pitch + line, 8, stride=pitch), :], back, 0))
        return [blend(turned[a], turned[(a + 1) % 8], 8 - shift) for a in range(LEVELS // 8)]

    for k in range(steps):
        for j in range(blocks):
            lanes = slice(j * LANES, (j + 1) * LANES)
            wide = slice(k * width + j * LANES, k * width + (j + 1) * LANES)
            real, imag = rows(k * lines + j), rows(k * lines + blocks + j)
            cos_row, sin_row = cos_row_ref[:, wide], sin_row_ref[:, wide]
            for a in range(LEVELS // 8):
                span = slice(8 * a, 8 * a + 8)
                cos_tile = cos_tile_ref[a : a + 1, wide]
                sin_tile = sin_tile_ref[a : a + 1, wide]
                cosine = cos_tile * cos_row - sin_tile * sin_row
                sine = sin_tile * cos_row + cos_tile * sin_row
                out_buf[k, 0, span, lanes] = cosine * real[a] - sine * imag[a]
                out_buf[k, 1, span, lanes] = sine * real[a] + cosine * imag[a]
        stores[k].start()
    moment_buf[0] = jnp.sum(tree([term[...] for term in term_refs])) / total
    moment.start()
    moment.wait()
    for store in stores:
        store.wait()


def butterfly(value, axis, last):
    size = lax.axis_size(axis)

    def partner(reach):
        return lax.ppermute(value, axis, [(i, i ^ reach) for i in range(size)])

    reach = 1
    while reach < size // last:
        value = value + partner(reach)
        reach *= 2
    return [value] + [partner(reach * i) for i in range(1, last)]


def tree(terms):
    while len(terms) > 1:
        terms = [terms[i] + terms[i + 1] for i in range(0, len(terms), 2)]
    return terms[0]


def local(state, sector_mix, kerr_rates, column_load):
    pair_count = lax.axis_size("pairs")
    col_devices = lax.axis_size("cols")
    device = lax.axis_index("pairs")
    col_device = lax.axis_index("cols")
    levels, col_count = state.shape[2], state.shape[3]
    assert pair_count == levels == LEVELS and state.shape[1] == 1
    state = state.reshape(2, levels, col_count)
    blocks = col_count // LANES
    lines = 2 * blocks
    part = blocks // STEPS
    width = part * LANES
    params = pltpu.CompilerParams(vmem_limit_bytes=VMEM_LIMIT)

    def exchange(rows):
        return lax.all_to_all(rows, "pairs", 0, 0, tiled=True)

    low = lax.dynamic_slice_in_dim(sector_mix, device, 1, 0)
    high = lax.dynamic_slice_in_dim(sector_mix, jnp.minimum(device + levels, 2 * levels - 2), 1, 0)
    mine = jnp.concatenate([low, high], 0)
    share = mine.shape[2]
    pieces = jnp.zeros((2, levels, LANES), jnp.float32)
    for step in range(col_devices):
        ring = [(i, (i + step) % col_devices) for i in range(col_devices)]
        received = lax.ppermute(mine, "cols", ring) if step else mine
        owner = (col_device - step) % col_devices
        pieces = lax.dynamic_update_slice(pieces, received, (0, 0, owner * share))

    anywhere = pl.BlockSpec(memory_space=pl.ANY)
    vmem = pl.BlockSpec(memory_space=pltpu.VMEM)
    rows_shape = pltpu.HBM((levels, lines, LANES), jnp.float32)
    rows_buf = pltpu.VMEM((STEPS, levels * 2 * part, LANES), jnp.float32)
    state_buf = pltpu.VMEM((STEPS, 2, levels, width), jnp.float32)
    sems = pltpu.SemaphoreType.DMA((STEPS,))

    packed = pl.pallas_call(
        pack_kernel,
        in_specs=[anywhere],
        out_specs=anywhere,
        out_shape=rows_shape,
        scratch_shapes=[state_buf, rows_buf, sems, sems],
        compiler_params=params,
        name="pack",
    )(pltpu.with_memory_space_constraint(state, pltpu.HBM))
    arrived = exchange(packed)

    n1 = device.astype(jnp.float32)
    eight = jnp.arange(8).astype(jnp.float32)
    loads = column_load.astype(jnp.float32)[None, :]
    tile_phases = (kerr_rates[0] * n1 + kerr_rates[1] * (8.0 * eight))[:, None] * loads
    row_phases = (kerr_rates[1] * eight)[:, None] * loads
    tables = (jnp.cos(tile_phases), jnp.sin(tile_phases), jnp.cos(row_phases), jnp.sin(row_phases))
    matrix = pl.pallas_call(
        matrix_kernel,
        in_specs=[vmem],
        out_specs=vmem,
        out_shape=jax.ShapeDtypeStruct((levels, 3 * levels), jnp.bfloat16),
        compiler_params=params,
        name="matrix",
    )(pieces)
    arrived, tables, matrix = lax.optimization_barrier((arrived, tables, matrix))

    mixed, moment = pl.pallas_call(
        functools.partial(mix_kernel, col_count),
        in_specs=[vmem, vmem],
        out_specs=[anywhere, vmem],
        out_shape=[rows_shape, jax.ShapeDtypeStruct((1, LANES), jnp.float32)],
        scratch_shapes=[rows_buf, sems],
        compiler_params=params,
        name="mix",
    )(arrived, matrix)
    returned = exchange(mixed)

    terms = butterfly(tree(butterfly(moment, "cols", 2)), "pairs", 8)
    total = float(levels * levels * col_count * col_devices * levels * THIRD)

    evolved, moment = pl.pallas_call(
        functools.partial(turn_kernel, total),
        in_specs=[vmem] * (5 + len(terms)),
        out_specs=[anywhere, anywhere],
        out_shape=[pltpu.HBM((2, levels, col_count), jnp.float32), pltpu.HBM((1,), jnp.float32)],
        scratch_shapes=[state_buf, pltpu.SMEM((1,), jnp.float32), sems, pltpu.SemaphoreType.DMA],
        compiler_params=params,
        name="turn",
    )(returned, *tables, *terms)
    return evolved.reshape(2, 1, levels, col_count), moment


def solution(mesh):
    placed = (P(None, "pairs", None, "cols"), P(None, None, "cols"), P(), P("cols"))
    return jax.shard_map(
        local,
        mesh=mesh,
        in_specs=placed,
        out_specs=(P(None, "pairs", None, "cols"), P()),
        check_vma=False,
    )
```

```python
import functools

import jax
import jax.numpy as jnp
from jax import lax
from jax.experimental import pallas as pl
from jax.experimental.pallas import tpu as pltpu
from jax.sharding import PartitionSpec as P

THIRD = 64
MEMB = 128
WINDOW = 2
LEVELS = 64
LANES = 128
STEPS = 8
VMEM_LIMIT = 24 * 1024 * 1024


def blend(low, high, shift):
    sub = lax.broadcasted_iota(jnp.int32, low.shape, 0)
    return jnp.where(sub < shift, low, high)


def pack_kernel(x_ref, out_ref, x_buf, out_buf, in_sem, out_sem):
    steps, lines = out_buf.shape[0], out_buf.shape[1] // LEVELS
    width = lines * LANES
    groups = x_ref.shape[2] // width
    n1 = lax.axis_index("pairs")
    tile, shift = n1 // 8, n1 % 8
    loads = [
        pltpu.make_async_copy(x_ref.at[k // groups, :, pl.ds(k % groups * width, width)], x_buf.at[k], in_sem.at[k])
        for k in range(steps)
    ]
    stores = [
        pltpu.make_async_copy(
            out_buf.at[k].reshape(LEVELS, lines, LANES), out_ref.at[:, pl.ds(k * lines, lines), :], out_sem.at[k]
        )
        for k in range(steps)
    ]
    for load in loads:
        load.start()
    for k in range(steps):
        loads[k].wait()
        for j in range(lines):
            lanes = slice(j * LANES, (j + 1) * LANES)
            turned = [pltpu.roll(x_buf[k, 8 * a : 8 * a + 8, lanes], shift, 0) for a in range(LEVELS // 8)]
            for a in range(LEVELS // 8):
                slot = 8 * ((a + tile) % 8)
                out_buf[k, pl.ds(slot * lines + j, 8, stride=lines), :] = blend(turned[a - 1], turned[a], shift)
        stores[k].start()
    for store in stores:
        store.wait()


def split(values):
    high = values.astype(jnp.bfloat16)
    return high, (values - high.astype(jnp.float32)).astype(jnp.bfloat16)


def matrix_kernel(pieces_ref, matrix_ref):
    owner = lax.axis_index("pairs")
    row = lax.broadcasted_iota(jnp.int32, (LEVELS, LANES), 0)
    col = lax.broadcasted_iota(jnp.int32, (LEVELS, LANES), 1)
    low = pieces_ref[0]
    high = pltpu.roll(pltpu.roll(pieces_ref[1], owner + 1, 0), owner + 1, 1)
    zero = jnp.zeros_like(low)
    low = jnp.where((row <= owner) & (col <= owner), low, zero)
    high = jnp.where((row > owner) & (col > owner) & (col < LEVELS), high, zero)
    top, rest = split((low + high)[:, :LEVELS])
    matrix_ref[...] = jnp.concatenate([top, top, rest], 1)


def mix_kernel(col_count, x_ref, matrix_ref, out_ref, moment_ref, out_buf, out_sem):
    steps, lines = out_buf.shape[0], out_buf.shape[1] // LEVELS
    blocks = lines // 2
    pitch = steps * lines
    source = x_ref.reshape(LEVELS * pitch, LANES)
    stores = [
        pltpu.make_async_copy(
            out_buf.at[k].reshape(LEVELS, lines, LANES), out_ref.at[:, pl.ds(k * lines, lines), :], out_sem.at[k]
        )
        for k in range(steps)
    ]
    base = lax.axis_index("cols") * (col_count // (MEMB * WINDOW))
    row = lax.broadcasted_iota(jnp.int32, (LEVELS, LANES), 0)
    matrix = matrix_ref[...]
    total = jnp.zeros((LEVELS, LANES), jnp.float32)
    for k in range(steps):
        for line in range(0, lines, 2):
            top, rest = split(
                jnp.concatenate([source[pl.ds(k * lines + line + i, LEVELS, stride=pitch), :] for i in range(2)], 1)
            )
            mixed = jnp.dot(matrix, jnp.concatenate([top, rest, top], 0), preferred_element_type=jnp.float32)
            for i in range(2):
                out = mixed[:, i * LANES : (i + 1) * LANES]
                out_buf[k, pl.ds(line + i, LEVELS, stride=lines), :] = out
                third = base + (k * lines + line + i) * LANES % col_count // (MEMB * WINDOW)
                total += (third + 1).astype(jnp.float32) * (out * out)
        stores[k].start()
    moment_ref[...] = jnp.sum(total * (row + 1).astype(jnp.float32), axis=0, keepdims=True)
    for store in stores:
        store.wait()


def turn_kernel(total, x_ref, cos_tile_ref, sin_tile_ref, cos_row_ref, sin_row_ref, *refs):
    *term_refs, out_ref, moment_ref, out_buf, moment_buf, out_sem, moment_sem = refs
    moment = pltpu.make_async_copy(moment_buf, moment_ref, moment_sem)
    steps, width = out_buf.shape[0], out_buf.shape[3]
    blocks = width // LANES
    lines = 2 * blocks
    pitch = steps * lines
    flat = x_ref.reshape(LEVELS * pitch, LANES)
    n1 = lax.axis_index("pairs")
    tile, shift = n1 // 8, n1 % 8
    back = (8 - shift) % 8
    stores = [
        pltpu.make_async_copy(out_buf.at[k], out_ref.at[:, :, pl.ds(k * width, width)], out_sem.at[k])
        for k in range(steps)
    ]

    def rows(line):
        turned = []
        for a in range(LEVELS // 8):
            slot = 8 * ((a + tile) % 8)
            turned.append(pltpu.roll(flat[pl.ds(slot * pitch + line, 8, stride=pitch), :], back, 0))
        return [blend(turned[a], turned[(a + 1) % 8], 8 - shift) for a in range(LEVELS // 8)]

    for k in range(steps):
        for j in range(blocks):
            lanes = slice(j * LANES, (j + 1) * LANES)
            wide = slice(k * width + j * LANES, k * width + (j + 1) * LANES)
            real, imag = rows(k * blocks + j), rows((steps + k) * blocks + j)
            cos_row, sin_row = cos_row_ref[:, wide], sin_row_ref[:, wide]
            for a in range(LEVELS // 8):
                span = slice(8 * a, 8 * a + 8)
                cos_tile = cos_tile_ref[a : a + 1, wide]
                sin_tile = sin_tile_ref[a : a + 1, wide]
                cosine = cos_tile * cos_row - sin_tile * sin_row
                sine = sin_tile * cos_row + cos_tile * sin_row
                out_buf[k, 0, span, lanes] = cosine * real[a] - sine * imag[a]
                out_buf[k, 1, span, lanes] = sine * real[a] + cosine * imag[a]
        stores[k].start()
        if k == 0:
            moment_buf[0] = jnp.sum(tree([term[...] for term in term_refs])) / total
            moment.start()
    moment.wait()
    for store in stores:
        store.wait()


def butterfly(value, axis, last):
    size = lax.axis_size(axis)

    def partner(reach):
        return lax.ppermute(value, axis, [(i, i ^ reach) for i in range(size)])

    reach = 1
    while reach < size // last:
        value = value + partner(reach)
        reach *= 2
    return [value] + [partner(reach * i) for i in range(1, last)]


def tree(terms):
    while len(terms) > 1:
        terms = [terms[i] + terms[i + 1] for i in range(0, len(terms), 2)]
    return terms[0]


def local(state, sector_mix, kerr_rates, column_load):
    pair_count = lax.axis_size("pairs")
    col_devices = lax.axis_size("cols")
    device = lax.axis_index("pairs")
    col_device = lax.axis_index("cols")
    levels, col_count = state.shape[2], state.shape[3]
    assert pair_count == levels == LEVELS and state.shape[1] == 1
    state = state.reshape(2, levels, col_count)
    blocks = col_count // LANES
    lines = 2 * blocks
    part = blocks // STEPS
    width = part * LANES
    params = pltpu.CompilerParams(vmem_limit_bytes=VMEM_LIMIT)

    def exchange(rows):
        return lax.all_to_all(rows, "pairs", 0, 0, tiled=True)

    low = lax.dynamic_slice_in_dim(sector_mix, device, 1, 0)
    high = lax.dynamic_slice_in_dim(sector_mix, jnp.minimum(device + levels, 2 * levels - 2), 1, 0)
    mine = jnp.concatenate([low, high], 0)
    share = mine.shape[2]
    pieces = jnp.zeros((2, levels, LANES), jnp.float32)
    for step in range(col_devices):
        ring = [(i, (i + step) % col_devices) for i in range(col_devices)]
        received = lax.ppermute(mine, "cols", ring) if step else mine
        owner = (col_device - step) % col_devices
        pieces = lax.dynamic_update_slice(pieces, received, (0, 0, owner * share))

    anywhere = pl.BlockSpec(memory_space=pl.ANY)
    vmem = pl.BlockSpec(memory_space=pltpu.VMEM)
    rows_shape = pltpu.HBM((levels, lines, LANES), jnp.float32)
    rows_buf = pltpu.VMEM((STEPS, levels * 2 * part, LANES), jnp.float32)
    state_buf = pltpu.VMEM((STEPS, 2, levels, width), jnp.float32)
    sems = pltpu.SemaphoreType.DMA((STEPS,))

    packed = pl.pallas_call(
        pack_kernel,
        in_specs=[anywhere],
        out_specs=anywhere,
        out_shape=rows_shape,
        scratch_shapes=[pltpu.VMEM((STEPS, levels, 2 * width), jnp.float32), rows_buf, sems, sems],
        compiler_params=params,
        name="pack",
    )(pltpu.with_memory_space_constraint(state, pltpu.HBM))
    arrived = exchange(packed)

    n1 = device.astype(jnp.float32)
    eight = jnp.arange(8).astype(jnp.float32)
    loads = column_load.astype(jnp.float32)[None, :]
    tile_phases = (kerr_rates[0] * n1 + kerr_rates[1] * (8.0 * eight))[:, None] * loads
    row_phases = (kerr_rates[1] * eight)[:, None] * loads
    tables = (jnp.cos(tile_phases), jnp.sin(tile_phases), jnp.cos(row_phases), jnp.sin(row_phases))
    matrix = pl.pallas_call(
        matrix_kernel,
        in_specs=[vmem],
        out_specs=vmem,
        out_shape=jax.ShapeDtypeStruct((levels, 3 * levels), jnp.bfloat16),
        compiler_params=params,
        name="matrix",
    )(pieces)
    arrived, tables, matrix = lax.optimization_barrier((arrived, tables, matrix))

    mixed, moment = pl.pallas_call(
        functools.partial(mix_kernel, col_count),
        in_specs=[vmem, vmem],
        out_specs=[anywhere, vmem],
        out_shape=[rows_shape, jax.ShapeDtypeStruct((1, LANES), jnp.float32)],
        scratch_shapes=[rows_buf, sems],
        compiler_params=params,
        name="mix",
    )(arrived, matrix)
    returned = exchange(mixed)

    terms = butterfly(tree(butterfly(moment, "cols", 2)), "pairs", 8)
    total = float(levels * levels * col_count * col_devices * levels * THIRD)

    evolved, moment = pl.pallas_call(
        functools.partial(turn_kernel, total),
        in_specs=[vmem] * (5 + len(terms)),
        out_specs=[anywhere, anywhere],
        out_shape=[pltpu.HBM((2, levels, col_count), jnp.float32), pltpu.HBM((1,), jnp.float32)],
        scratch_shapes=[state_buf, pltpu.SMEM((1,), jnp.float32), sems, pltpu.SemaphoreType.DMA],
        compiler_params=params,
        name="turn",
    )(returned, *tables, *terms)
    return evolved.reshape(2, 1, levels, col_count), moment


def solution(mesh):
    placed = (P(None, "pairs", None, "cols"), P(None, None, "cols"), P(), P("cols"))
    return jax.shard_map(
        local,
        mesh=mesh,
        in_specs=placed,
        out_specs=(P(None, "pairs", None, "cols"), P()),
        check_vma=False,
    )
```
